512 devices in a mesh: agg: 32 (over x, y), grp: 16 (over z, core).
Axes of the slice: x: 4, y: 8, z: 8, core: 2. Of those that a mesh axis runs over, the one named last changes fastest.
Arguments:
- a_blocks: bfloat16 [32, 16, 16, 5, 128, 128], P('agg', 'grp'), may hold values from -0.5 to 0.5
- a_cols: int32 [32, 16, 16, 5], P('agg', 'grp'), may hold values from 0 to 23, as said below
- p_blocks: bfloat16 [32, 16, 16, 2, 128, 128], P('agg', 'grp'), may hold values from -0.5 to 0.5
- p_cols: int32 [32, 16, 16, 2], P(None, 'grp'), may hold values from 0 to 2, as said below
Outputs:
- coarse_matrix: bfloat16 [32, 128, 3, 9, 128], P('agg')
The draws below stay inside these ranges and needn't reach their ends.
Inputs may be any that keep to these rules, and one draw needn't show every extreme that they name: `a_cols`: slot 0 of row r is 4 + r. In every region but the first, slot 1 of the rows r < 4 names a row 0 to 4 - 1 (row 0 names 0); in every region but the last, slot 4 of the rows r >= 12 names a row 20 to 16 + 2 * 4 - 1 (row 15 names the last). All other slots name rows 4 to 19; a row may name a column more than once. `p_cols`: the 2 entries of a row are 2 consecutive coarse rows counted modulo 3, all different. Every index of agg holds the whole array.
All inputs are finite; a program needn't handle non-finite values.
Results may differ from the reference program's by a relative error of at most 0.025.
Values may be sent and summed in bfloat16 or wider, within the bound.
No kernel may reach another device: no remote copies, remote signals or barrier semaphores. Data moves between devices by JAX's collectives and lax.ppermute only.
A program may use at most 64 MiB of HBM per device.

```python
import jax
import jax.numpy as jnp
from jax import lax

B = 128
FR = 16
KA = 5
KP = 2
NC = 3
HB = 4
REGIONS = 32
MEMBERS = 16


def draw_a_cols(key, part):
    full_shape = (REGIONS, MEMBERS, FR, KA)
    own_rows = HB + jax.random.randint(jax.random.fold_in(key, 11), full_shape, 0, FR)
    behind_rows = jax.random.randint(jax.random.fold_in(key, 12), full_shape, 0, HB)
    ahead_rows = HB + FR + jax.random.randint(jax.random.fold_in(key, 13), full_shape, 0, HB)
    region_index = lax.broadcasted_iota(jnp.int32, full_shape, 0)
    row_index = lax.broadcasted_iota(jnp.int32, full_shape, 2)
    slot_index = lax.broadcasted_iota(jnp.int32, full_shape, 3)
    behind_rows = jnp.where(row_index == 0, 0, behind_rows)
    ahead_rows = jnp.where(row_index == FR - 1, FR + 2 * HB - 1, ahead_rows)
    columns = jnp.where(slot_index == 0, HB + row_index, own_rows)
    columns = jnp.where((slot_index == 1) & (row_index < HB) & (region_index > 0), behind_rows, columns)
    columns = jnp.where((slot_index == KA - 1) & (row_index >= FR - HB) & (region_index < REGIONS - 1), ahead_rows, columns)
    return columns.astype(jnp.int32)


def draw_p_cols(key, part):
    full_shape = (REGIONS, MEMBERS, FR, KP)
    offsets = jax.random.randint(jax.random.fold_in(key, 21), (REGIONS, MEMBERS, FR, 1), 0, NC)
    first_index = lax.broadcasted_iota(jnp.int32, (REGIONS, MEMBERS, FR, 1), 0)
    second_index = lax.broadcasted_iota(jnp.int32, (REGIONS, MEMBERS, FR, 1), 1)
    third_index = lax.broadcasted_iota(jnp.int32, (REGIONS, MEMBERS, FR, 1), 2)
    leading = (first_index == 0) & (second_index == 0) & (third_index == 0)
    offsets = jnp.where(leading, NC - 1, offsets)
    slot_index = lax.broadcasted_iota(jnp.int32, full_shape, 3)
    return ((offsets + slot_index) % NC).astype(jnp.int32)


def block_scale(rng, dims, cuts, least, largest):
    gain, own = 1.0, jax.random.fold_in(rng, 6)
    for position, shards_of in cuts:
        steps = jnp.exp(jax.random.uniform(jax.random.fold_in(own, position), (shards_of,), jnp.float32, least / len(cuts), largest / len(cuts)))
        gain = gain * jnp.repeat(steps, dims[position] // shards_of).reshape([-1 if axis == position else 1 for axis in range(len(dims))])
    return gain


def centred(key, shape, deviation, bound, cuts=(), kind=jnp.bfloat16):
    gain = block_scale(key, shape, cuts, -0.22, 0.18) if cuts else 1.0
    entries = jax.random.normal(key, shape, jnp.float32) * deviation * gain
    return jnp.minimum(jnp.maximum(entries, -bound), bound).astype(kind)


def setup_inputs(seed: int = 0) -> dict:
    keys = jax.random.split(jax.random.key(seed), 5)
    a_blocks = centred(keys[0], (REGIONS, MEMBERS, FR, KA, B, B), B ** -0.5, 0.5, ((0, 32), (1, 16)))
    a_cols = draw_a_cols(jax.random.fold_in(keys[4], 71), 0)
    p_blocks = centred(keys[2], (REGIONS, MEMBERS, FR, KP, B, B), B ** -0.5, 0.5, ((0, 32), (1, 16)))
    p_cols = draw_p_cols(jax.random.fold_in(keys[4], 71), 0)
    return dict(a_blocks=a_blocks, a_cols=a_cols, p_blocks=p_blocks, p_cols=p_cols)


def device_term(a_here, col_here, p_ext_here, ids_ext_here, p_here, pc_here):
    band = 3 * NC
    targets = NC * band
    taken = p_ext_here[col_here]
    applied = jnp.einsum('rkxy,rkmyz->rkmxz', a_here.astype(jnp.float32), taken.astype(jnp.float32))
    applied = applied.astype(jnp.bfloat16).reshape(FR, KA * KP, B, B)
    slot_ids = ids_ext_here[col_here].reshape(FR, KA * KP)
    pieces = jnp.einsum('rnxy,rsxz->rnsyz', p_here.astype(jnp.float32), applied.astype(jnp.float32))
    target_ids = (pc_here[:, :, None] * band + slot_ids[:, None, :]).reshape(-1).astype(jnp.int32)
    summed = jax.ops.segment_sum(pieces.reshape(-1, B, B), target_ids, num_segments=targets)
    rounded = lax.optimization_barrier(summed.astype(jnp.bfloat16))
    return rounded.astype(jnp.float32)


def reference(a_blocks, a_cols, p_blocks, p_cols):
    band = 3 * NC
    targets = NC * band
    zero_rim = jnp.zeros((1, MEMBERS, HB, KP, B, B), p_blocks.dtype)
    behind = jnp.concatenate([zero_rim, p_blocks[:-1, :, FR - HB:]], 0)
    ahead = jnp.concatenate([p_blocks[1:, :, :HB], zero_rim], 0)
    p_extended = jnp.concatenate([behind, p_blocks, ahead], 2)
    zero_ids = jnp.zeros((1, MEMBERS, HB, KP), jnp.int32)
    ids_behind = jnp.concatenate([zero_ids, p_cols[:-1, :, FR - HB:]], 0)
    ids_ahead = jnp.concatenate([p_cols[1:, :, :HB], zero_ids], 0) + 2 * NC
    ids_extended = jnp.concatenate([ids_behind, p_cols + NC, ids_ahead], 2).astype(jnp.int32)

    def region_matrix(index):
        def add_member(total, member):
            term = device_term(a_blocks[index][member], a_cols[index][member], p_extended[index][member], ids_extended[index][member], p_blocks[index][member], p_cols[index][member])
            return total + term, None

        total, _ = lax.scan(add_member, jnp.zeros((targets, B, B), jnp.float32), jnp.arange(MEMBERS, dtype=jnp.int32))
        return total.astype(jnp.bfloat16).transpose(1, 0, 2).reshape(B, NC, band, B)

    return lax.map(region_matrix, jnp.arange(REGIONS, dtype=jnp.int32))
```

```python
import functools

import jax
import jax.numpy as jnp
from jax import lax
from jax.experimental import pallas as pl
from jax.experimental.pallas import tpu as pltpu
from jax.sharding import Mesh
from jax.sharding import PartitionSpec as P

NC = 3
HB = 4
F32 = jnp.float32
BF16 = jnp.bfloat16


def contract_rows(a, b):
    return lax.dot_general(a, b, (((0,), (0,)), ((), ())), preferred_element_type=F32)


def own_kernel(fr, ka, b, acol, pcol, a, p, own, w_lo, w_hi, routed, grouped):
    region = lax.axis_index("agg")
    zeros = jnp.zeros((b, b), BF16)
    for d in range(NC):
        routed[d, pl.ds(fr * b, b), :] = zeros
    for r in range(fr):
        first, second = pcol[2 * r, region], pcol[2 * r + 1, region]
        rows = pl.ds(r * b, b)
        routed[first, rows, :] = p[r, 0]
        routed[second, rows, :] = p[r, 1]
        routed[NC - first - second, rows, :] = zeros

    def block_row(start):
        rows = pl.ds(pl.multiple_of(start, b), b)
        return jnp.concatenate([routed[d, rows, :] for d in range(NC)], axis=1)

    for r in range(fr):
        starts = []
        for k in range(ka):
            col = acol[k, r]
            own_row = (col >= HB) & (col < HB + fr)
            starts.append(jnp.where(own_row, col - HB, fr) * b)
        left = jnp.concatenate([a[r, k] for k in range(ka)], axis=1)
        right = jnp.concatenate([block_row(s) for s in starts], axis=0)
        g = jnp.dot(left, right, preferred_element_type=F32)
        grouped[pl.ds(r * b, b), :] = g.astype(BF16)
    every = jnp.concatenate([routed[d, pl.ds(0, fr * b), :] for d in range(NC)], axis=1)
    own[...] = contract_rows(every, grouped[...]).astype(BF16)

    for out, first_row, slot, least in ((w_lo, 0, 1, None), (w_hi, fr - HB, ka - 1, HB + fr)):
        for i in range(HB):
            r = first_row + i
            col = acol[slot, r]
            outside = col < HB if least is None else col >= least
            w = contract_rows(block_row(r * b), a[r, slot])
            out[:, pl.ds(i * b, b)] = jnp.where(outside, w, 0.0).astype(BF16)


def halo_kernel(fr, ka, b, pieces, regions, acol, pcol, own, w_lo, w_hi, lo, hi, keep, send, routed):
    region = lax.axis_index("agg")
    core = lax.axis_index("core")
    zeros = jnp.zeros((b, b), BF16)
    band = 3 * NC
    per = NC * band * b // pieces

    def halo_part(w, halo, first_row, slot, base, source, source_row):
        for i in range(HB):
            j = jnp.clip(acol[slot, first_row + i] - base, 0, HB - 1)
            at = 2 * (source_row + j)
            first, second = pcol[at, source], pcol[at + 1, source]
            rows = pl.ds(i * b, b)
            routed[first, rows, :] = halo[j, 0]
            routed[second, rows, :] = halo[j, 1]
            routed[NC - first - second, rows, :] = zeros
        right = jnp.concatenate([routed[d] for d in range(NC)], axis=1)
        return jnp.dot(w[...], right, preferred_element_type=F32).astype(BF16)

    parts = [
        halo_part(w_lo, lo, 0, 1, 0, jnp.maximum(region - 1, 0), fr - HB),
        own[...],
        halo_part(w_hi, hi, fr - HB, ka - 1, HB + fr, jnp.minimum(region + 1, regions - 1), 0),
    ]

    def write(even, odd):
        for c in range(NC):
            for d in range(band):
                block = parts[d // NC][c * b : (c + 1) * b, (d % NC) * b : (d % NC + 1) * b]
                at = (c * band + d) * b
                done = 0
                while done < b:
                    q, offset = divmod(at + done, per)
                    count = min(b - done, per - offset)
                    (even, odd)[q % 2][q // 2, offset : offset + count, :] = block[done : done + count]
                    done += count

    @pl.when(core == 0)
    def _():
        write(keep, send)

    @pl.when(core == 1)
    def _():
        write(send, keep)


def body(a_blocks, a_cols, p_blocks, p_cols):
    a_local, p_local = a_blocks[0, 0], p_blocks[0, 0]
    fr, ka, b = a_local.shape[:3]
    regions = p_cols.shape[0]
    acol = a_cols[0, 0].T
    pcol = p_cols[:, 0].transpose(1, 2, 0).reshape(fr * 2, regions)
    band = 3 * NC
    z_count, core_count = lax.axis_size("z"), lax.axis_size("core")
    pieces = z_count * core_count
    per = NC * band * b // pieces
    forward = [(i, i + 1) for i in range(regions - 1)]
    backward = [(target, source) for source, target in forward]
    lo = lax.ppermute(p_local[fr - HB :], "agg", forward)
    hi = lax.ppermute(p_local[:HB], "agg", backward)

    vmem = pl.BlockSpec(memory_space=pltpu.VMEM)
    smem = pl.BlockSpec(memory_space=pltpu.SMEM)
    n = NC * b
    own, w_lo, w_hi = pl.pallas_call(
        functools.partial(own_kernel, fr, ka, b),
        out_shape=[
            jax.ShapeDtypeStruct((n, n), BF16),
            jax.ShapeDtypeStruct((n, HB * b), BF16),
            jax.ShapeDtypeStruct((n, HB * b), BF16),
        ],
        in_specs=[smem, smem, vmem, vmem],
        out_specs=[vmem] * 3,
        scratch_shapes=[
            pltpu.VMEM((NC, (fr + 1) * b, b), BF16),
            pltpu.VMEM((fr * b, n), BF16),
        ],
        cost_estimate=pl.CostEstimate(flops=2_000_000_000, bytes_accessed=6_000_000, transcendentals=0),
        compiler_params=pltpu.CompilerParams(vmem_limit_bytes=40 << 20),
        name="own_part",
    )(acol, pcol, a_local, p_local)

    keep, send = pl.pallas_call(
        functools.partial(halo_kernel, fr, ka, b, pieces, regions),
        out_shape=[jax.ShapeDtypeStruct((z_count, per, b), BF16)] * 2,
        in_specs=[smem, smem] + [vmem] * 5,
        out_specs=[vmem] * 2,
        scratch_shapes=[pltpu.VMEM((NC, HB * b, b), BF16)],
        cost_estimate=pl.CostEstimate(flops=400_000_000, bytes_accessed=3_000_000, transcendentals=0),
        compiler_params=pltpu.CompilerParams(vmem_limit_bytes=20 << 20),
        name="halo_part",
    )(acol, pcol, own, w_lo, w_hi, lo, hi)

    got = lax.ppermute(send, "core", [(0, 1), (1, 0)])
    pair = (keep.astype(F32) + got.astype(F32)).astype(BF16)
    mine = lax.all_to_all(pair, "z", 0, 0, tiled=True)
    mine = mine.astype(F32).sum(0).astype(BF16)
    whole = lax.all_gather(mine, ("z", "core"), tiled=True)
    return whole.reshape(NC, band, b, b).transpose(2, 0, 1, 3)[None]


def solution(mesh):
    agg, grp = mesh.devices.shape
    split = Mesh(mesh.devices.reshape(agg, grp // 2, 2), ("agg", "z", "core"))
    both = ("z", "core")
    return jax.shard_map(
        body,
        mesh=split,
        in_specs=(
            P("agg", both, None, None, None, None),
            P("agg", both, None, None),
            P("agg", both, None, None, None, None),
            P(None, both, None, None),
        ),
        out_specs=P("agg", None, None, None, None),
        check_vma=False,
    )
```

```python
import functools

import jax
import jax.numpy as jnp
from jax import lax
from jax.experimental import pallas as pl
from jax.experimental.pallas import tpu as pltpu
from jax.sharding import Mesh
from jax.sharding import PartitionSpec as P

NC = 3
HB = 4
F32 = jnp.float32
BF16 = jnp.bfloat16


def contract_rows(a, b):
    return lax.dot_general(a, b, (((0,), (0,)), ((), ())), preferred_element_type=F32)


def own_kernel(fr, ka, b, chunks, acol_hbm, pcol_hbm, a_hbm, p_hbm, own, v_lo, v_hi, mask, acol, pcol, a, p, routed, grouped, summed, sems):
    region = lax.axis_index("agg")
    last = lax.axis_size("agg") - 1
    step = fr // chunks
    copies = [
        pltpu.make_async_copy(pcol_hbm, pcol, sems.at[0]),
        pltpu.make_async_copy(p_hbm, p, sems.at[1]),
        pltpu.make_async_copy(acol_hbm, acol, sems.at[2]),
    ]
    for i in range(chunks):
        rows = pl.ds(i * step, step)
        copies.append(pltpu.make_async_copy(a_hbm.at[rows], a.at[rows], sems.at[3 + i]))
    for copy in copies:
        copy.start()

    zeros = jnp.zeros((b, b), BF16)
    for d in range(NC):
        routed[d, pl.ds(fr * b, b), :] = zeros
    copies[0].wait()
    mask[...] = jnp.zeros_like(mask)
    one = jnp.ones(mask.shape[-2:], BF16)
    for side, source, first_row in ((0, jnp.maximum(region - 1, 0), fr - HB), (1, jnp.minimum(region + 1, last), 0)):
        for j in range(HB):
            for m in range(2):
                mask[side, j, m, pcol[first_row + j, m, source]] = one
    copies[1].wait()
    for r in range(fr):
        first, second = pcol[r, 0, region], pcol[r, 1, region]
        rows = pl.ds(r * b, b)
        routed[first, rows, :] = p[r, 0]
        routed[second, rows, :] = p[r, 1]
        routed[NC - first - second, rows, :] = zeros
    copies[2].wait()

    def block_row(start):
        rows = pl.ds(pl.multiple_of(start, b), b)
        return jnp.concatenate([routed[d, rows, :] for d in range(NC)], axis=1)

    for r in range(fr):
        if r % step == 0:
            copies[3 + r // step].wait()
        starts = []
        for k in range(ka):
            col = acol[k, 0, r]
            own_row = (col >= HB) & (col < HB + fr)
            starts.append(jnp.where(own_row, col - HB, fr) * b)
        left = jnp.concatenate([a[r, k] for k in range(ka)], axis=1)
        right = jnp.concatenate([block_row(s) for s in starts], axis=0)
        g = jnp.dot(left, right, preferred_element_type=F32)
        grouped[pl.ds(r * b, b), :] = g.astype(BF16)
    every = jnp.concatenate([routed[d, pl.ds(0, fr * b), :] for d in range(NC)], axis=1)
    own[...] = contract_rows(every, grouped[...]).astype(BF16)

    for out, first_row, slot, base in ((v_lo, 0, 1, 0), (v_hi, fr - HB, ka - 1, HB + fr)):
        summed[...] = jnp.zeros_like(summed)
        for i in range(HB):
            r = first_row + i
            j = acol[slot, 0, r] - base

            @pl.when((j >= 0) & (j < HB))
            def _(r=r, j=j, slot=slot):
                summed[jnp.clip(j, 0, HB - 1)] += contract_rows(block_row(r * b), a[r, slot])

        for j in range(HB):
            out[:, pl.ds(j * b, b)] = summed[j].astype(BF16)


def halo_kernel(b, pieces, own, v_lo, v_hi, mask, lo, hi, keep, send):
    core = lax.axis_index("core")
    band = 3 * NC
    per = NC * band * b // pieces
    tile = mask.shape[-2]

    def halo_part(side, v, halo):
        columns = []
        for d in range(NC):
            rows = []
            for j in range(HB):
                terms = [halo[j, m].reshape(b // tile, tile, b) * mask[side, j, m, d][None] for m in range(2)]
                rows.append((terms[0] + terms[1]).reshape(b, b))
            columns.append(jnp.concatenate(rows, axis=0))
        right = jnp.concatenate(columns, axis=1)
        return jnp.dot(v[...], right, preferred_element_type=F32).astype(BF16)

    parts = [halo_part(0, v_lo, lo), own[...], halo_part(1, v_hi, hi)]

    def write(even, odd):
        for c in range(NC):
            for d in range(band):
                block = parts[d // NC][c * b : (c + 1) * b, (d % NC) * b : (d % NC + 1) * b]
                at = (c * band + d) * b
                done = 0
                while done < b:
                    q, offset = divmod(at + done, per)
                    count = min(b - done, per - offset)
                    (even, odd)[q % 2][q // 2, offset : offset + count, :] = block[done : done + count]
                    done += count

    @pl.when(core == 0)
    def _():
        write(keep, send)

    @pl.when(core == 1)
    def _():
        write(send, keep)


def body(a_blocks, a_cols, p_blocks, p_cols):
    a_local, p_local = a_blocks[0, 0], p_blocks[0, 0]
    fr, ka, b = a_local.shape[:3]
    regions = p_cols.shape[0]
    acol = a_cols[0].transpose(2, 0, 1)
    pcol = p_cols[:, 0].transpose(1, 2, 0)
    band = 3 * NC
    chunks = 4
    z_count, core_count = lax.axis_size("z"), lax.axis_size("core")
    pieces = z_count * core_count
    per = NC * band * b // pieces
    forward = [(i, i + 1) for i in range(regions - 1)]
    backward = [(target, source) for source, target in forward]
    lo = lax.ppermute(p_local[fr - HB :], "agg", forward)
    hi = lax.ppermute(p_local[:HB], "agg", backward)

    vmem = pl.BlockSpec(memory_space=pltpu.VMEM)
    hbm = pl.BlockSpec(memory_space=pltpu.HBM)
    n = NC * b
    own, v_lo, v_hi, mask = pl.pallas_call(
        functools.partial(own_kernel, fr, ka, b, chunks),
        out_shape=[
            jax.ShapeDtypeStruct((n, n), BF16),
            jax.ShapeDtypeStruct((n, HB * b), BF16),
            jax.ShapeDtypeStruct((n, HB * b), BF16),
            jax.ShapeDtypeStruct((2, HB, 2, NC, 16, b), BF16),
        ],
        in_specs=[hbm] * 4,
        out_specs=[vmem] * 4,
        scratch_shapes=[
            pltpu.SMEM(acol.shape, jnp.int32),
            pltpu.SMEM(pcol.shape, jnp.int32),
            pltpu.VMEM(a_local.shape, BF16),
            pltpu.VMEM(p_local.shape, BF16),
            pltpu.VMEM((NC, (fr + 1) * b, b), BF16),
            pltpu.VMEM((fr * b, n), BF16),
            pltpu.VMEM((HB, n, b), F32),
            pltpu.SemaphoreType.DMA((3 + chunks,)),
        ],
        cost_estimate=pl.CostEstimate(flops=2_000_000_000, bytes_accessed=6_000_000, transcendentals=0),
        compiler_params=pltpu.CompilerParams(vmem_limit_bytes=40 << 20),
        name="own_part",
    )(*[pltpu.with_memory_space_constraint(x, pltpu.HBM) for x in (acol, pcol, a_local, p_local)])

    keep, send = pl.pallas_call(
        functools.partial(halo_kernel, b, pieces),
        out_shape=[jax.ShapeDtypeStruct((z_count, per, b), BF16)] * 2,
        in_specs=[vmem] * 6,
        out_specs=[vmem] * 2,
        cost_estimate=pl.CostEstimate(flops=400_000_000, bytes_accessed=3_000_000, transcendentals=0),
        compiler_params=pltpu.CompilerParams(vmem_limit_bytes=20 << 20),
        name="halo_part",
    )(own, v_lo, v_hi, mask, lo, hi)

    sent = lax.all_gather(send, "core")
    got = lax.dynamic_index_in_dim(sent, 1 - lax.axis_index("core"), 0, keepdims=False)
    pair = (keep.astype(F32) + got.astype(F32)).astype(BF16)
    mine = lax.all_to_all(pair, "z", 0, 0, tiled=True)
    mine = mine.astype(F32).sum(0).astype(BF16)
    whole = lax.all_gather(mine, ("z", "core"), tiled=True)
    return whole.reshape(NC, band, b, b).transpose(2, 0, 1, 3)[None]


def solution(mesh):
    agg, grp = mesh.devices.shape
    split = Mesh(mesh.devices.reshape(agg, grp // 2, 2), ("agg", "z", "core"))
    both = ("z", "core")
    return jax.shard_map(
        body,
        mesh=split,
        in_specs=(
            P("agg", both, None, None, None, None),
            P("agg", both, None, None),
            P("agg", both, None, None, None, None),
            P(None, both, None, None),
        ),
        out_specs=P("agg", None, None, None, None),
        check_vma=False,
    )
```

```python
import functools

import jax
import jax.numpy as jnp
from jax import lax
from jax.experimental import pallas as pl
from jax.experimental.pallas import tpu as pltpu
from jax.sharding import PartitionSpec as P

NC = 3
HB = 4
F32 = jnp.float32
BF16 = jnp.bfloat16


def contract_rows(a, b):
    return lax.dot_general(a, b, (((0,), (0,)), ((), ())), preferred_element_type=F32)


def own_kernel(fr, ka, b, chunks, acol_hbm, pcol_hbm, a_hbm, p_hbm, own, v_first, v_second, mask, acol, pcol, a, p, routed, grouped, summed, sems):
    region = lax.axis_index("agg")
    last = lax.axis_size("agg") - 1
    step = fr // chunks
    copies = [
        pltpu.make_async_copy(pcol_hbm, pcol, sems.at[0]),
        pltpu.make_async_copy(p_hbm, p, sems.at[1]),
        pltpu.make_async_copy(acol_hbm, acol, sems.at[2]),
    ]
    for i in range(chunks):
        rows = pl.ds(i * step, step)
        copies.append(pltpu.make_async_copy(a_hbm.at[rows], a.at[rows], sems.at[3 + i]))
    for copy in copies:
        copy.start()

    zeros = jnp.zeros((b, b), BF16)
    for d in range(NC):
        routed[d, pl.ds(fr * b, b), :] = zeros
    copies[0].wait()
    mask[...] = jnp.zeros_like(mask)
    one = jnp.ones(mask.shape[-2:], BF16)
    odd = lax.rem(region, 2)
    for side in range(2):
        low = odd == 1 - side
        source = jnp.where(low, jnp.maximum(region - 1, 0), jnp.minimum(region + 1, last))
        first_row = jnp.where(low, fr - HB, 0)
        for j in range(HB):
            for m in range(2):
                mask[side, j, m, pcol[first_row + j, m, source]] = one
    copies[1].wait()
    for r in range(fr):
        first, second = pcol[r, 0, region], pcol[r, 1, region]
        rows = pl.ds(r * b, b)
        routed[first, rows, :] = p[r, 0]
        routed[second, rows, :] = p[r, 1]
        routed[NC - first - second, rows, :] = zeros
    copies[2].wait()

    def block_row(start):
        rows = pl.ds(pl.multiple_of(start, b), b)
        return jnp.concatenate([routed[d, rows, :] for d in range(NC)], axis=1)

    for r in range(fr):
        if r % step == 0:
            copies[3 + r // step].wait()
        starts = []
        for k in range(ka):
            col = acol[k, 0, r]
            own_row = (col >= HB) & (col < HB + fr)
            starts.append(jnp.where(own_row, col - HB, fr) * b)
        left = jnp.concatenate([a[r, k] for k in range(ka)], axis=1)
        right = jnp.concatenate([block_row(s) for s in starts], axis=0)
        g = jnp.dot(left, right, preferred_element_type=F32)
        grouped[pl.ds(r * b, b), :] = g.astype(BF16)
    every = jnp.concatenate([routed[d, pl.ds(0, fr * b), :] for d in range(NC)], axis=1)
    own[...] = contract_rows(every, grouped[...]).astype(BF16)

    for side, out in enumerate((v_first, v_second)):
        low = odd == 1 - side
        first_row, slot, base = jnp.where(low, 0, fr - HB), jnp.where(low, 1, ka - 1), jnp.where(low, 0, HB + fr)
        summed[...] = jnp.zeros_like(summed)
        for i in range(HB):
            r = first_row + i
            j = acol[slot, 0, r] - base

            @pl.when((j >= 0) & (j < HB))
            def _(r=r, j=j, slot=slot):
                summed[jnp.clip(j, 0, HB - 1)] += contract_rows(block_row(r * b), a[r, slot])

        for j in range(HB):
            out[:, pl.ds(j * b, b)] = summed[j].astype(BF16)


def halo_kernel(b, pieces, own, v_first, v_second, mask, first, second, keep, send):
    core = lax.rem(lax.axis_index("grp"), 2)
    odd = lax.rem(lax.axis_index("agg"), 2) == 1
    band = 3 * NC
    per = NC * band * b // pieces
    tile = mask.shape[-2]

    def halo_part(side, v, halo):
        columns = []
        for d in range(NC):
            rows = []
            for j in range(HB):
                terms = [halo[j, m].reshape(b // tile, tile, b) * mask[side, j, m, d][None] for m in range(2)]
                rows.append((terms[0] + terms[1]).reshape(b, b))
            columns.append(jnp.concatenate(rows, axis=0))
        right = jnp.concatenate(columns, axis=1)
        return jnp.dot(v[...], right, preferred_element_type=F32).astype(BF16)

    by_first, by_second = halo_part(0, v_first, first), halo_part(1, v_second, second)
    parts = [jnp.where(odd, by_first, by_second), own[...], jnp.where(odd, by_second, by_first)]

    def write(even_core, odd_core):
        for c in range(NC):
            for d in range(band):
                block = parts[d // NC][c * b : (c + 1) * b, (d % NC) * b : (d % NC + 1) * b]
                at = (c * band + d) * b
                done = 0
                while done < b:
                    q, offset = divmod(at + done, per)
                    count = min(b - done, per - offset)
                    (even_core, odd_core)[q % 2][pieces // 2 - 1 - q // 2, offset : offset + count, :] = block[done : done + count]
                    done += count

    @pl.when(core == 0)
    def _():
        write(keep, send)

    @pl.when(core == 1)
    def _():
        write(send, keep)


def body(a_blocks, a_cols, p_blocks, p_cols):
    a_local, p_local = a_blocks[0, 0], p_blocks[0, 0]
    fr, ka, b = a_local.shape[:3]
    regions = p_cols.shape[0]
    acol = a_cols[0].transpose(2, 0, 1)
    pcol = p_cols[:, 0].transpose(1, 2, 0)
    band = 3 * NC
    chunks = 4
    pieces = lax.axis_size("grp")
    z_count = pieces // 2
    per = NC * band * b // pieces
    odd = lax.rem(lax.axis_index("agg"), 2)

    def swap(least, start):
        pairs = [(i, i + 1) for i in range(least, regions - 1, 2)]
        ends = lax.dynamic_slice_in_dim(p_local, start * (fr - HB), HB, 0)
        return lax.ppermute(ends, "agg", pairs + [(j, i) for i, j in pairs])

    first, second = swap(0, 1 - odd), swap(1, odd)

    vmem = pl.BlockSpec(memory_space=pltpu.VMEM)
    hbm = pl.BlockSpec(memory_space=pltpu.HBM)
    n = NC * b
    own, v_first, v_second, mask = pl.pallas_call(
        functools.partial(own_kernel, fr, ka, b, chunks),
        out_shape=[
            jax.ShapeDtypeStruct((n, n), BF16),
            jax.ShapeDtypeStruct((n, HB * b), BF16),
            jax.ShapeDtypeStruct((n, HB * b), BF16),
            jax.ShapeDtypeStruct((2, HB, 2, NC, 16, b), BF16),
        ],
        in_specs=[hbm] * 4,
        out_specs=[vmem] * 4,
        scratch_shapes=[
            pltpu.SMEM(acol.shape, jnp.int32),
            pltpu.SMEM(pcol.shape, jnp.int32),
            pltpu.VMEM(a_local.shape, BF16),
            pltpu.VMEM(p_local.shape, BF16),
            pltpu.VMEM((NC, (fr + 1) * b, b), BF16),
            pltpu.VMEM((fr * b, n), BF16),
            pltpu.VMEM((HB, n, b), F32),
            pltpu.SemaphoreType.DMA((3 + chunks,)),
        ],
        cost_estimate=pl.CostEstimate(flops=2_000_000_000, bytes_accessed=6_000_000, transcendentals=0),
        compiler_params=pltpu.CompilerParams(vmem_limit_bytes=40 << 20),
        name="own_part",
    )(*[pltpu.with_memory_space_constraint(x, pltpu.HBM) for x in (acol, pcol, a_local, p_local)])

    keep, send = pl.pallas_call(
        functools.partial(halo_kernel, b, pieces),
        out_shape=[jax.ShapeDtypeStruct((z_count, per, b), BF16)] * 2,
        in_specs=[vmem] * 6,
        out_specs=[vmem] * 2,
        cost_estimate=pl.CostEstimate(flops=400_000_000, bytes_accessed=3_000_000, transcendentals=0),
        compiler_params=pltpu.CompilerParams(vmem_limit_bytes=20 << 20),
        name="halo_part",
    )(own, v_first, v_second, mask, first, second)

    chips = [[2 * z, 2 * z + 1] for z in range(z_count)]
    same_core = [[2 * z + c for z in range(z_count)] for c in range(2)]
    falling = [[2 * z + c for z in reversed(range(z_count)) for c in range(2)]]
    sent = lax.all_gather(send, "grp", axis_index_groups=chips)
    core = lax.rem(lax.axis_index("grp"), 2)
    got = lax.dynamic_index_in_dim(sent, 1 - core, 0, keepdims=False)
    pair = (keep.astype(F32) + got.astype(F32)).astype(BF16)
    mine = lax.all_to_all(pair, "grp", 0, 0, tiled=True, axis_index_groups=same_core)
    mine = mine.astype(F32).sum(0).astype(BF16)
    whole = lax.all_gather(mine, "grp", tiled=True, axis_index_groups=falling)
    return whole.reshape(NC, band, b, b).transpose(2, 0, 1, 3)[None]


def solution(mesh):
    return jax.shard_map(
        body,
        mesh=mesh,
        in_specs=(
            P("agg", "grp", None, None, None, None),
            P("agg", "grp", None, None),
            P("agg", "grp", None, None, None, None),
            P(None, "grp", None, None),
        ),
        out_specs=P("agg", None, None, None, None),
        check_vma=False,
    )
```

```python
import functools

import jax
import jax.numpy as jnp
from jax import lax
from jax.experimental import pallas as pl
from jax.experimental.pallas import tpu as pltpu
from jax.sharding import PartitionSpec as P

NC = 3
HB = 4
F32 = jnp.float32
BF16 = jnp.bfloat16


def contract_rows(a, b):
    return lax.dot_general(a, b, (((0,), (0,)), ((), ())), preferred_element_type=F32)


def own_kernel(fr, ka, b, chunks, acol_hbm, pcol_hbm, a_hbm, p_hbm, own, v_first, v_second, mask, acol, pcol, a, p, routed, grouped, sems):
    region = lax.axis_index("agg")
    last = lax.axis_size("agg") - 1
    step = fr // chunks
    copies = [
        pltpu.make_async_copy(pcol_hbm, pcol, sems.at[0]),
        pltpu.make_async_copy(p_hbm, p, sems.at[1]),
        pltpu.make_async_copy(acol_hbm, acol, sems.at[2]),
    ]
    for i in range(chunks):
        rows = pl.ds(i * step, step)
        copies.append(pltpu.make_async_copy(a_hbm.at[rows], a.at[rows], sems.at[3 + i]))
    for copy in copies:
        copy.start()

    zeros = jnp.zeros((b, b), BF16)
    for d in range(NC):
        routed[d, pl.ds(fr * b, b), :] = zeros
    copies[0].wait()
    mask[...] = jnp.zeros_like(mask)
    one = jnp.ones(mask.shape[-2:], BF16)
    odd = lax.rem(region, 2)
    for side in range(2):
        low = odd == 1 - side
        source = jnp.where(low, jnp.maximum(region - 1, 0), jnp.minimum(region + 1, last))
        first_row = jnp.where(low, fr - HB, 0)
        for j in range(HB):
            for m in range(2):
                mask[side, j, m, pcol[first_row + j, m, source]] = one
    copies[1].wait()
    for r in range(fr):
        first, second = pcol[r, 0, region], pcol[r, 1, region]
        rows = pl.ds(r * b, b)
        routed[first, rows, :] = p[r, 0]
        routed[second, rows, :] = p[r, 1]
        routed[NC - first - second, rows, :] = zeros
    copies[2].wait()

    def block_row(start):
        rows = pl.ds(pl.multiple_of(start, b), b)
        return jnp.concatenate([routed[d, rows, :] for d in range(NC)], axis=1)

    for r in range(fr):
        if r % step == 0:
            copies[3 + r // step].wait()
        starts = []
        for k in range(ka):
            col = acol[k, 0, r]
            own_row = (col >= HB) & (col < HB + fr)
            starts.append(jnp.where(own_row, col - HB, fr) * b)
        left = jnp.concatenate([a[r, k] for k in range(ka)], axis=1)
        right = jnp.concatenate([block_row(s) for s in starts], axis=0)
        g = jnp.dot(left, right, preferred_element_type=F32)
        grouped[pl.ds(r * b, b), :] = g.astype(BF16)
    every = jnp.concatenate([routed[d, pl.ds(0, fr * b), :] for d in range(NC)], axis=1)
    own[...] = contract_rows(every, grouped[...]).astype(BF16)

    for side, out in enumerate((v_first, v_second)):
        low = odd == 1 - side
        first_row, slot, base = jnp.where(low, 0, fr - HB), jnp.where(low, 1, ka - 1), jnp.where(low, 0, HB + fr)
        rows = []
        for i in range(HB):
            r = first_row + i
            block = a[r, slot]
            j = acol[slot, 0, r] - base
            rows.append(jnp.concatenate([jnp.where(j == t, block, zeros) for t in range(HB)], axis=1))
        here = pl.ds(pl.multiple_of(first_row * b, b), HB * b)
        left = jnp.concatenate([routed[d, here, :] for d in range(NC)], axis=1)
        out[...] = contract_rows(left, jnp.concatenate(rows, axis=0)).astype(BF16)


def halo_kernel(b, pieces, own, v_first, v_second, mask, first, second, keep, send):
    core = lax.rem(lax.axis_index("grp"), 2)
    odd = lax.rem(lax.axis_index("agg"), 2) == 1
    band = 3 * NC
    per = NC * band * b // pieces
    tile = mask.shape[-2]

    def halo_part(side, v, halo):
        columns = []
        for d in range(NC):
            rows = []
            for j in range(HB):
                terms = [halo[j, m].reshape(b // tile, tile, b) * mask[side, j, m, d][None] for m in range(2)]
                rows.append((terms[0] + terms[1]).reshape(b, b))
            columns.append(jnp.concatenate(rows, axis=0))
        right = jnp.concatenate(columns, axis=1)
        return jnp.dot(v[...], right, preferred_element_type=F32).astype(BF16)

    by_first, by_second = halo_part(0, v_first, first), halo_part(1, v_second, second)
    parts = [jnp.where(odd, by_first, by_second), own[...], jnp.where(odd, by_second, by_first)]

    def write(even_core, odd_core):
        for c in range(NC):
            for d in range(band):
                block = parts[d // NC][c * b : (c + 1) * b, (d % NC) * b : (d % NC + 1) * b]
                at = (c * band + d) * b
                done = 0
                while done < b:
                    q, offset = divmod(at + done, per)
                    count = min(b - done, per - offset)
                    at_slot = pieces // 2 - 1 - q // 2 if q % 2 else q // 2
                    (even_core, odd_core)[q % 2][at_slot, offset : offset + count, :] = block[done : done + count]
                    done += count

    @pl.when(core == 0)
    def _():
        write(keep, send)

    @pl.when(core == 1)
    def _():
        write(send, keep)


def first_kernel(a_local, a_cols, p_local, p_cols):
    fr, ka, b = a_local.shape[:3]
    acol = a_cols[0].transpose(2, 0, 1)
    pcol = p_cols[:, 0].transpose(1, 2, 0)
    chunks = 4
    vmem = pl.BlockSpec(memory_space=pltpu.VMEM)
    hbm = pl.BlockSpec(memory_space=pltpu.HBM)
    n = NC * b
    return pl.pallas_call(
        functools.partial(own_kernel, fr, ka, b, chunks),
        out_shape=[
            jax.ShapeDtypeStruct((n, n), BF16),
            jax.ShapeDtypeStruct((n, HB * b), BF16),
            jax.ShapeDtypeStruct((n, HB * b), BF16),
            jax.ShapeDtypeStruct((2, HB, 2, NC, 16, b), BF16),
        ],
        in_specs=[hbm] * 4,
        out_specs=[vmem] * 4,
        scratch_shapes=[
            pltpu.SMEM(acol.shape, jnp.int32),
            pltpu.SMEM(pcol.shape, jnp.int32),
            pltpu.VMEM(a_local.shape, BF16),
            pltpu.VMEM(p_local.shape, BF16),
            pltpu.VMEM((NC, (fr + 1) * b, b), BF16),
            pltpu.VMEM((fr * b, n), BF16),
            pltpu.SemaphoreType.DMA((3 + chunks,)),
        ],
        cost_estimate=pl.CostEstimate(flops=2_000_000_000, bytes_accessed=6_000_000, transcendentals=0),
        compiler_params=pltpu.CompilerParams(vmem_limit_bytes=40 << 20),
        name="own_part",
    )(*[pltpu.with_memory_space_constraint(x, pltpu.HBM) for x in (acol, pcol, a_local, p_local)])


def body(a_blocks, a_cols, p_blocks, p_cols):
    a_local, p_local = a_blocks[0, 0], p_blocks[0, 0]
    fr, ka, b = a_local.shape[:3]
    regions = p_cols.shape[0]
    band = 3 * NC
    pieces = lax.axis_size("grp")
    z_count = pieces // 2
    per = NC * band * b // pieces
    odd = lax.rem(lax.axis_index("agg"), 2)

    def swap(least, start):
        pairs = [(i, i + 1) for i in range(least, regions - 1, 2)]
        ends = lax.dynamic_slice_in_dim(p_local, start * (fr - HB), HB, 0)
        return lax.ppermute(ends, "agg", pairs + [(j, i) for i, j in pairs])

    first, second = swap(0, 1 - odd), swap(1, odd)

    vmem = pl.BlockSpec(memory_space=pltpu.VMEM)
    own, v_first, v_second, mask = first_kernel(a_local, a_cols, p_local, p_cols)

    keep, send = pl.pallas_call(
        functools.partial(halo_kernel, b, pieces),
        out_shape=[jax.ShapeDtypeStruct((z_count, per, b), BF16)] * 2,
        in_specs=[vmem] * 6,
        out_specs=[vmem] * 2,
        cost_estimate=pl.CostEstimate(flops=400_000_000, bytes_accessed=3_000_000, transcendentals=0),
        compiler_params=pltpu.CompilerParams(vmem_limit_bytes=20 << 20),
        name="halo_part",
    )(own, v_first, v_second, mask, first, second)

    chips = [[2 * z, 2 * z + 1] for z in range(z_count)]
    same_core = [[2 * z for z in reversed(range(z_count))], [2 * z + 1 for z in range(z_count)]]
    falling = [[2 * z + c for z in reversed(range(z_count)) for c in range(2)]]
    sent = lax.all_gather(send, "grp", axis_index_groups=chips)
    core = lax.rem(lax.axis_index("grp"), 2)
    got = lax.dynamic_index_in_dim(sent, 1 - core, 0, keepdims=False)
    pair = (keep.astype(F32) + got.astype(F32)).astype(BF16)
    mine = lax.all_to_all(pair, "grp", 0, 0, tiled=True, axis_index_groups=same_core)
    mine = mine.astype(F32).sum(0).astype(BF16)
    whole = lax.all_gather(mine, "grp", tiled=True, axis_index_groups=falling)
    return whole.reshape(NC, band, b, b).transpose(2, 0, 1, 3)[None]


def solution(mesh):
    return jax.shard_map(
        body,
        mesh=mesh,
        in_specs=(
            P("agg", "grp", None, None, None, None),
            P("agg", "grp", None, None),
            P("agg", "grp", None, None, None, None),
            P(None, "grp", None, None),
        ),
        out_specs=P("agg", None, None, None, None),
        check_vma=False,
    )
```

```python
import functools

import jax
import jax.numpy as jnp
from jax import lax
from jax.experimental import pallas as pl
from jax.experimental.pallas import tpu as pltpu
from jax.sharding import PartitionSpec as P

NC = 3
HB = 4
F32 = jnp.float32
BF16 = jnp.bfloat16


def contract_rows(a, b):
    return lax.dot_general(a, b, (((0,), (0,)), ((), ())), preferred_element_type=F32)


def own_kernel(fr, ka, b, chunks, acol_hbm, pcol_hbm, a_hbm, p_hbm, own, v_first, v_second, mask, acol, pcol, a, p, routed, grouped, sems):
    region = lax.axis_index("agg")
    last = lax.axis_size("agg") - 1
    step = fr // chunks
    copies = [
        pltpu.make_async_copy(pcol_hbm, pcol, sems.at[0]),
        pltpu.make_async_copy(p_hbm, p, sems.at[1]),
        pltpu.make_async_copy(acol_hbm, acol, sems.at[2]),
    ]
    for i in range(chunks):
        rows = pl.ds(i * step, step)
        copies.append(pltpu.make_async_copy(a_hbm.at[rows], a.at[rows], sems.at[3 + i]))
    for copy in copies:
        copy.start()

    zeros = jnp.zeros((b, b), BF16)
    for d in range(NC):
        routed[d, pl.ds(fr * b, b), :] = zeros
    copies[0].wait()
    mask[...] = jnp.zeros_like(mask)
    one = jnp.ones(mask.shape[-2:], BF16)
    odd = lax.rem(region + lax.axis_index("grp"), 2)
    for side in range(2):
        low = odd == 1 - side
        source = jnp.where(low, jnp.maximum(region - 1, 0), jnp.minimum(region + 1, last))
        first_row = jnp.where(low, fr - HB, 0)
        for j in range(HB):
            for m in range(2):
                mask[side, j, m, pcol[first_row + j, m, source]] = one
    copies[1].wait()
    for r in range(fr):
        first, second = pcol[r, 0, region], pcol[r, 1, region]
        rows = pl.ds(r * b, b)
        routed[first, rows, :] = p[r, 0]
        routed[second, rows, :] = p[r, 1]
        routed[NC - first - second, rows, :] = zeros
    copies[2].wait()

    def block_row(start):
        rows = pl.ds(pl.multiple_of(start, b), b)
        return jnp.concatenate([routed[d, rows, :] for d in range(NC)], axis=1)

    for r in range(fr):
        if r % step == 0:
            copies[3 + r // step].wait()
        starts = []
        for k in range(ka):
            col = acol[k, 0, r]
            own_row = (col >= HB) & (col < HB + fr)
            starts.append(jnp.where(own_row, col - HB, fr) * b)
        left = jnp.concatenate([a[r, k] for k in range(ka)], axis=1)
        right = jnp.concatenate([block_row(s) for s in starts], axis=0)
        g = jnp.dot(left, right, preferred_element_type=F32)
        grouped[pl.ds(r * b, b), :] = g.astype(BF16)
    every = jnp.concatenate([routed[d, pl.ds(0, fr * b), :] for d in range(NC)], axis=1)
    own[...] = contract_rows(every, grouped[...]).astype(BF16)

    for side, out in enumerate((v_first, v_second)):
        low = odd == 1 - side
        first_row, slot, base = jnp.where(low, 0, fr - HB), jnp.where(low, 1, ka - 1), jnp.where(low, 0, HB + fr)
        rows = []
        for i in range(HB):
            r = first_row + i
            block = a[r, slot]
            j = acol[slot, 0, r] - base
            rows.append(jnp.concatenate([jnp.where(j == t, block, zeros) for t in range(HB)], axis=1))
        here = pl.ds(pl.multiple_of(first_row * b, b), HB * b)
        left = jnp.concatenate([routed[d, here, :] for d in range(NC)], axis=1)
        out[...] = contract_rows(left, jnp.concatenate(rows, axis=0)).astype(BF16)


def halo_kernel(b, pieces, own, v_first, v_second, mask, first, second, keep, send):
    core = lax.rem(lax.axis_index("grp"), 2)
    odd = lax.rem(lax.axis_index("agg") + lax.axis_index("grp"), 2) == 1
    band = 3 * NC
    per = NC * band * b // pieces
    tile = mask.shape[-2]

    def halo_part(side, v, halo):
        columns = []
        for d in range(NC):
            rows = []
            for j in range(HB):
                terms = [halo[j, m].reshape(b // tile, tile, b) * mask[side, j, m, d][None] for m in range(2)]
                rows.append((terms[0] + terms[1]).reshape(b, b))
            columns.append(jnp.concatenate(rows, axis=0))
        right = jnp.concatenate(columns, axis=1)
        return jnp.dot(v[...], right, preferred_element_type=F32).astype(BF16)

    by_first, by_second = halo_part(0, v_first, first), halo_part(1, v_second, second)
    parts = [jnp.where(odd, by_first, by_second), own[...], jnp.where(odd, by_second, by_first)]

    def write(even_core, odd_core):
        for c in range(NC):
            for d in range(band):
                block = parts[d // NC][c * b : (c + 1) * b, (d % NC) * b : (d % NC + 1) * b]
                at = (c * band + d) * b
                done = 0
                while done < b:
                    q, offset = divmod(at + done, per)
                    count = min(b - done, per - offset)
                    at_slot = pieces // 2 - 1 - q // 2 if q % 2 else q // 2
                    (even_core, odd_core)[q % 2][at_slot, offset : offset + count, :] = block[done : done + count]
                    done += count

    @pl.when(core == 0)
    def _():
        write(keep, send)

    @pl.when(core == 1)
    def _():
        write(send, keep)


def first_kernel(a_local, a_cols, p_local, p_cols):
    fr, ka, b = a_local.shape[:3]
    acol = a_cols[0].transpose(2, 0, 1)
    pcol = p_cols[:, 0].transpose(1, 2, 0)
    chunks = 4
    vmem = pl.BlockSpec(memory_space=pltpu.VMEM)
    hbm = pl.BlockSpec(memory_space=pltpu.HBM)
    n = NC * b
    return pl.pallas_call(
        functools.partial(own_kernel, fr, ka, b, chunks),
        out_shape=[
            jax.ShapeDtypeStruct((n, n), BF16),
            jax.ShapeDtypeStruct((n, HB * b), BF16),
            jax.ShapeDtypeStruct((n, HB * b), BF16),
            jax.ShapeDtypeStruct((2, HB, 2, NC, 16, b), BF16),
        ],
        in_specs=[hbm] * 4,
        out_specs=[vmem] * 4,
        scratch_shapes=[
            pltpu.SMEM(acol.shape, jnp.int32),
            pltpu.SMEM(pcol.shape, jnp.int32),
            pltpu.VMEM(a_local.shape, BF16),
            pltpu.VMEM(p_local.shape, BF16),
            pltpu.VMEM((NC, (fr + 1) * b, b), BF16),
            pltpu.VMEM((fr * b, n), BF16),
            pltpu.SemaphoreType.DMA((3 + chunks,)),
        ],
        cost_estimate=pl.CostEstimate(flops=2_000_000_000, bytes_accessed=6_000_000, transcendentals=0),
        compiler_params=pltpu.CompilerParams(vmem_limit_bytes=40 << 20),
        name="own_part",
    )(*[pltpu.with_memory_space_constraint(x, pltpu.HBM) for x in (acol, pcol, a_local, p_local)])


def body(a_blocks, a_cols, p_blocks, p_cols):
    a_local, p_local = a_blocks[0, 0], p_blocks[0, 0]
    fr, ka, b = a_local.shape[:3]
    regions = p_cols.shape[0]
    band = 3 * NC
    pieces = lax.axis_size("grp")
    z_count = pieces // 2
    per = NC * band * b // pieces
    odd = lax.rem(lax.axis_index("agg") + lax.axis_index("grp"), 2)

    def swap(least, start):
        pairs = [
            (i * pieces + g, (i + 1) * pieces + g)
            for g in range(pieces)
            for i in range((least + g) % 2, regions - 1, 2)
        ]
        ends = lax.dynamic_slice_in_dim(p_local, start * (fr - HB), HB, 0)
        return lax.ppermute(ends, ("agg", "grp"), pairs + [(j, i) for i, j in pairs])

    first, second = swap(0, 1 - odd), swap(1, odd)

    vmem = pl.BlockSpec(memory_space=pltpu.VMEM)
    own, v_first, v_second, mask = first_kernel(a_local, a_cols, p_local, p_cols)

    keep, send = pl.pallas_call(
        functools.partial(halo_kernel, b, pieces),
        out_shape=[jax.ShapeDtypeStruct((z_count, per, b), BF16)] * 2,
        in_specs=[vmem] * 6,
        out_specs=[vmem] * 2,
        cost_estimate=pl.CostEstimate(flops=400_000_000, bytes_accessed=3_000_000, transcendentals=0),
        compiler_params=pltpu.CompilerParams(vmem_limit_bytes=20 << 20),
        name="halo_part",
    )(own, v_first, v_second, mask, first, second)

    chips = [[2 * z, 2 * z + 1] for z in range(z_count)]
    same_core = [[2 * z for z in reversed(range(z_count))], [2 * z + 1 for z in range(z_count)]]
    falling = [[2 * z + c for z in reversed(range(z_count)) for c in range(2)]]
    sent = lax.all_gather(send, "grp", axis_index_groups=chips)
    core = lax.rem(lax.axis_index("grp"), 2)
    got = lax.dynamic_index_in_dim(sent, 1 - core, 0, keepdims=False)
    pair = (keep.astype(F32) + got.astype(F32)).astype(BF16)
    mine = lax.all_to_all(pair, "grp", 0, 0, tiled=True, axis_index_groups=same_core)
    mine = mine.astype(F32).sum(0).astype(BF16)
    whole = lax.all_gather(mine, "grp", tiled=True, axis_index_groups=falling)
    return whole.reshape(NC, band, b, b).transpose(2, 0, 1, 3)[None]


def solution(mesh):
    return jax.shard_map(
        body,
        mesh=mesh,
        in_specs=(
            P("agg", "grp", None, None, None, None),
            P("agg", "grp", None, None),
            P("agg", "grp", None, None, None, None),
            P(None, "grp", None, None),
        ),
        out_specs=P("agg", None, None, None, None),
        check_vma=False,
    )
```

```python
import functools

import jax
import jax.numpy as jnp
from jax import lax
from jax.experimental import pallas as pl
from jax.experimental.pallas import tpu as pltpu
from jax.sharding import PartitionSpec as P

NC = 3
HB = 4
F32 = jnp.float32
BF16 = jnp.bfloat16


def contract_rows(a, b):
    return lax.dot_general(a, b, (((0,), (0,)), ((), ())), preferred_element_type=F32)


def own_kernel(fr, ka, b, chunks, acol_hbm, pcol_hbm, a_hbm, p_hbm, own, v_first, v_second, mask, acol, pcol, a, p, routed, grouped, sems):
    region = lax.axis_index("agg")
    last = lax.axis_size("agg") - 1
    step = fr // chunks
    copies = [
        pltpu.make_async_copy(pcol_hbm, pcol, sems.at[0]),
        pltpu.make_async_copy(p_hbm, p, sems.at[1]),
        pltpu.make_async_copy(acol_hbm, acol, sems.at[2]),
    ]
    for i in range(chunks):
        rows = pl.ds(i * step, step)
        copies.append(pltpu.make_async_copy(a_hbm.at[rows], a.at[rows], sems.at[3 + i]))
    for copy in copies[: 3 + 1]:
        copy.start()

    zeros = jnp.zeros((b, b), BF16)
    for d in range(NC):
        routed[d, pl.ds(fr * b, b), :] = zeros
    copies[0].wait()
    for copy in copies[3 + 1 :]:
        copy.start()
    mask[...] = jnp.zeros_like(mask)
    one = jnp.ones(mask.shape[-2:], BF16)
    odd = lax.rem(region + lax.axis_index("grp"), 2)
    for side in range(2):
        low = odd == 1 - side
        source = jnp.where(low, jnp.maximum(region - 1, 0), jnp.minimum(region + 1, last))
        first_row = jnp.where(low, fr - HB, 0)
        for j in range(HB):
            for m in range(2):
                mask[side, j, m, pcol[first_row + j, m, source]] = one
    copies[1].wait()
    for r in range(fr):
        first, second = pcol[r, 0, region], pcol[r, 1, region]
        rows = pl.ds(r * b, b)
        routed[first, rows, :] = p[r, 0]
        routed[second, rows, :] = p[r, 1]
        routed[NC - first - second, rows, :] = zeros
    copies[2].wait()

    def block_row(start):
        rows = pl.ds(pl.multiple_of(start, b), b)
        return jnp.concatenate([routed[d, rows, :] for d in range(NC)], axis=1)

    for r in range(fr):
        if r % step == 0:
            copies[3 + r // step].wait()
        starts = []
        for k in range(ka):
            col = acol[k, 0, r]
            own_row = (col >= HB) & (col < HB + fr)
            starts.append(jnp.where(own_row, col - HB, fr) * b)
        left = jnp.concatenate([a[r, k] for k in range(ka)], axis=1)
        right = jnp.concatenate([block_row(s) for s in starts], axis=0)
        g = jnp.dot(left, right, preferred_element_type=F32)
        grouped[pl.ds(r * b, b), :] = g.astype(BF16)
    every = jnp.concatenate([routed[d, pl.ds(0, fr * b), :] for d in range(NC)], axis=1)
    own[...] = contract_rows(every, grouped[...]).astype(BF16)

    for side, out in enumerate((v_first, v_second)):
        low = odd == 1 - side
        first_row, slot, base = jnp.where(low, 0, fr - HB), jnp.where(low, 1, ka - 1), jnp.where(low, 0, HB + fr)
        rows = []
        for i in range(HB):
            r = first_row + i
            block = a[r, slot]
            j = acol[slot, 0, r] - base
            rows.append(jnp.concatenate([jnp.where(j == t, block, zeros) for t in range(HB)], axis=1))
        here = pl.ds(pl.multiple_of(first_row * b, b), HB * b)
        left = jnp.concatenate([routed[d, here, :] for d in range(NC)], axis=1)
        out[...] = contract_rows(left, jnp.concatenate(rows, axis=0)).astype(BF16)


def halo_kernel(b, pieces, own, v_first, v_second, mask, first, second, keep, send):
    core = lax.rem(lax.axis_index("grp"), 2)
    odd = lax.rem(lax.axis_index("agg") + lax.axis_index("grp"), 2) == 1
    band = 3 * NC
    per = NC * band * b // pieces
    tile = mask.shape[-2]

    def halo_part(side, v, halo):
        columns = []
        for d in range(NC):
            rows = []
            for j in range(HB):
                terms = [halo[j, m].reshape(b // tile, tile, b) * mask[side, j, m, d][None] for m in range(2)]
                rows.append((terms[0] + terms[1]).reshape(b, b))
            columns.append(jnp.concatenate(rows, axis=0))
        right = jnp.concatenate(columns, axis=1)
        return jnp.dot(v[...], right, preferred_element_type=F32).astype(BF16)

    by_first, by_second = halo_part(0, v_first, first), halo_part(1, v_second, second)
    parts = [jnp.where(odd, by_first, by_second), own[...], jnp.where(odd, by_second, by_first)]

    def write(even_core, odd_core):
        for c in range(NC):
            for d in range(band):
                block = parts[d // NC][c * b : (c + 1) * b, (d % NC) * b : (d % NC + 1) * b]
                at = (c * band + d) * b
                done = 0
                while done < b:
                    q, offset = divmod(at + done, per)
                    count = min(b - done, per - offset)
                    at_slot = pieces // 2 - 1 - q // 2 if q % 2 else q // 2
                    (even_core, odd_core)[q % 2][at_slot, offset : offset + count, :] = block[done : done + count]
                    done += count

    @pl.when(core == 0)
    def _():
        write(keep, send)

    @pl.when(core == 1)
    def _():
        write(send, keep)


def first_kernel(a_local, a_cols, p_local, p_cols):
    fr, ka, b = a_local.shape[:3]
    acol = a_cols[0].transpose(2, 0, 1)
    pcol = p_cols[:, 0].transpose(1, 2, 0)
    chunks = 2
    vmem = pl.BlockSpec(memory_space=pltpu.VMEM)
    hbm = pl.BlockSpec(memory_space=pltpu.HBM)
    n = NC * b
    return pl.pallas_call(
        functools.partial(own_kernel, fr, ka, b, chunks),
        out_shape=[
            jax.ShapeDtypeStruct((n, n), BF16),
            jax.ShapeDtypeStruct((n, HB * b), BF16),
            jax.ShapeDtypeStruct((n, HB * b), BF16),
            jax.ShapeDtypeStruct((2, HB, 2, NC, 16, b), BF16),
        ],
        in_specs=[hbm] * 4,
        out_specs=[vmem] * 4,
        scratch_shapes=[
            pltpu.SMEM(acol.shape, jnp.int32),
            pltpu.SMEM(pcol.shape, jnp.int32),
            pltpu.VMEM(a_local.shape, BF16),
            pltpu.VMEM(p_local.shape, BF16),
            pltpu.VMEM((NC, (fr + 1) * b, b), BF16),
            pltpu.VMEM((fr * b, n), BF16),
            pltpu.SemaphoreType.DMA((3 + chunks,)),
        ],
        cost_estimate=pl.CostEstimate(flops=2_000_000_000, bytes_accessed=6_000_000, transcendentals=0),
        compiler_params=pltpu.CompilerParams(vmem_limit_bytes=40 << 20),
        name="own_part",
    )(*[pltpu.with_memory_space_constraint(x, pltpu.HBM) for x in (acol, pcol, a_local, p_local)])


def body(a_blocks, a_cols, p_blocks, p_cols):
    a_local, p_local = a_blocks[0, 0], p_blocks[0, 0]
    fr, ka, b = a_local.shape[:3]
    regions = p_cols.shape[0]
    band = 3 * NC
    pieces = lax.axis_size("grp")
    z_count = pieces // 2
    per = NC * band * b // pieces
    odd = lax.rem(lax.axis_index("agg") + lax.axis_index("grp"), 2)

    def swap(least, start):
        pairs = [
            (i * pieces + g, (i + 1) * pieces + g)
            for g in range(pieces)
            for i in range((least + g) % 2, regions - 1, 2)
        ]
        ends = lax.dynamic_slice_in_dim(p_local, start * (fr - HB), HB, 0)
        return lax.ppermute(ends, ("agg", "grp"), pairs + [(j, i) for i, j in pairs])

    first, second = swap(0, 1 - odd), swap(1, odd)

    vmem = pl.BlockSpec(memory_space=pltpu.VMEM)
    own, v_first, v_second, mask = first_kernel(a_local, a_cols, p_local, p_cols)

    keep, send = pl.pallas_call(
        functools.partial(halo_kernel, b, pieces),
        out_shape=[jax.ShapeDtypeStruct((z_count, per, b), BF16)] * 2,
        in_specs=[vmem] * 6,
        out_specs=[vmem] * 2,
        cost_estimate=pl.CostEstimate(flops=400_000_000, bytes_accessed=3_000_000, transcendentals=0),
        compiler_params=pltpu.CompilerParams(vmem_limit_bytes=20 << 20),
        name="halo_part",
    )(own, v_first, v_second, mask, first, second)

    chips = [[2 * z, 2 * z + 1] for z in range(z_count)]
    same_core = [[2 * z for z in reversed(range(z_count))], [2 * z + 1 for z in range(z_count)]]
    falling = [[2 * z + c for z in reversed(range(z_count)) for c in range(2)]]
    sent = lax.all_gather(send, "grp", axis_index_groups=chips)
    core = lax.rem(lax.axis_index("grp"), 2)
    got = lax.dynamic_index_in_dim(sent, 1 - core, 0, keepdims=False)
    pair = (keep.astype(F32) + got.astype(F32)).astype(BF16)
    mine = lax.all_to_all(pair, "grp", 0, 0, tiled=True, axis_index_groups=same_core)
    mine = mine.astype(F32).sum(0).astype(BF16)
    whole = lax.all_gather(mine, "grp", tiled=True, axis_index_groups=falling)
    return whole.reshape(NC, band, b, b).transpose(2, 0, 1, 3)[None]


def solution(mesh):
    return jax.shard_map(
        body,
        mesh=mesh,
        in_specs=(
            P("agg", "grp", None, None, None, None),
            P("agg", "grp", None, None),
            P("agg", "grp", None, None, None, None),
            P(None, "grp", None, None),
        ),
        out_specs=P("agg", None, None, None, None),
        check_vma=False,
    )
```

```python
import functools

import jax
import jax.numpy as jnp
from jax import lax
from jax.experimental import pallas as pl
from jax.experimental.pallas import tpu as pltpu
from jax.sharding import PartitionSpec as P

NC = 3
HB = 4
F32 = jnp.float32
BF16 = jnp.bfloat16


def contract_rows(a, b):
    return lax.dot_general(a, b, (((0,), (0,)), ((), ())), preferred_element_type=F32)


def own_kernel(fr, ka, b, chunks, acol_hbm, pcol_hbm, a_hbm, p_hbm, own, v_first, v_second, mask, acol, pcol, a, p, routed, grouped, sems):
    region = lax.axis_index("agg")
    last = lax.axis_size("agg") - 1
    step = fr // chunks
    copies = [
        pltpu.make_async_copy(pcol_hbm, pcol, sems.at[0]),
        pltpu.make_async_copy(p_hbm, p, sems.at[1]),
        pltpu.make_async_copy(acol_hbm, acol, sems.at[2]),
    ]
    for i in range(chunks):
        rows = pl.ds(i * step, step)
        copies.append(pltpu.make_async_copy(a_hbm.at[rows], a.at[rows], sems.at[3 + i]))
    for copy in copies[: 3 + 1]:
        copy.start()

    zeros = jnp.zeros((b, b), BF16)
    for d in range(NC):
        routed[d, pl.ds(fr * b, b), :] = zeros
    copies[0].wait()
    for copy in copies[3 + 1 :]:
        copy.start()
    mask[...] = jnp.zeros_like(mask)
    one = jnp.ones(mask.shape[-2:], BF16)
    odd = lax.rem(region + lax.axis_index("grp"), 2)
    for side in range(2):
        low = odd == 1 - side
        source = jnp.where(low, jnp.maximum(region - 1, 0), jnp.minimum(region + 1, last))
        first_row = jnp.where(low, fr - HB, 0)
        for j in range(HB):
            for m in range(2):
                mask[side, j, m, pcol[first_row + j, m, source]] = one
    copies[1].wait()
    for r in range(fr):
        first, second = pcol[r, 0, region], pcol[r, 1, region]
        rows = pl.ds(r * b, b)
        routed[first, rows, :] = p[r, 0]
        routed[second, rows, :] = p[r, 1]
        routed[NC - first - second, rows, :] = zeros
    copies[2].wait()

    def block_row(start):
        rows = pl.ds(pl.multiple_of(start, b), b)
        return jnp.concatenate([routed[d, rows, :] for d in range(NC)], axis=1)

    for r in range(fr):
        if r % step == 0:
            copies[3 + r // step].wait()
        starts = []
        for k in range(ka):
            col = acol[k, 0, r]
            own_row = (col >= HB) & (col < HB + fr)
            starts.append(jnp.where(own_row, col - HB, fr) * b)
        left = jnp.concatenate([a[r, k] for k in range(ka)], axis=1)
        right = jnp.concatenate([block_row(s) for s in starts], axis=0)
        g = jnp.dot(left, right, preferred_element_type=F32)
        grouped[pl.ds(r * b, b), :] = g.astype(BF16)
    for side, out in enumerate((v_first, v_second)):
        low = odd == 1 - side
        first_row, slot, base = jnp.where(low, 0, fr - HB), jnp.where(low, 1, ka - 1), jnp.where(low, 0, HB + fr)
        rows = []
        for i in range(HB):
            r = first_row + i
            block = a[r, slot]
            j = acol[slot, 0, r] - base
            rows.append(jnp.concatenate([jnp.where(j == t, block, zeros) for t in range(HB)], axis=1))
        here = pl.ds(pl.multiple_of(first_row * b, b), HB * b)
        left = jnp.concatenate([routed[d, here, :] for d in range(NC)], axis=1)
        out[...] = contract_rows(left, jnp.concatenate(rows, axis=0)).astype(BF16)

    every = jnp.concatenate([routed[d, pl.ds(0, fr * b), :] for d in range(NC)], axis=1)
    own[...] = contract_rows(every, grouped[...]).astype(BF16)


def halo_kernel(b, pieces, own, v_first, v_second, mask, first, second, keep, send):
    core = lax.rem(lax.axis_index("grp"), 2)
    odd = lax.rem(lax.axis_index("agg") + lax.axis_index("grp"), 2) == 1
    band = 3 * NC
    per = NC * band * b // pieces
    tile = mask.shape[-2]

    def halo_part(side, v, halo):
        columns = []
        for d in range(NC):
            rows = []
            for j in range(HB):
                terms = [halo[j, m].reshape(b // tile, tile, b) * mask[side, j, m, d][None] for m in range(2)]
                rows.append((terms[0] + terms[1]).reshape(b, b))
            columns.append(jnp.concatenate(rows, axis=0))
        right = jnp.concatenate(columns, axis=1)
        return jnp.dot(v[...], right, preferred_element_type=F32).astype(BF16)

    by_first, by_second = halo_part(0, v_first, first), halo_part(1, v_second, second)
    parts = [jnp.where(odd, by_first, by_second), own[...], jnp.where(odd, by_second, by_first)]

    def write(even_core, odd_core):
        for c in range(NC):
            for d in range(band):
                block = parts[d // NC][c * b : (c + 1) * b, (d % NC) * b : (d % NC + 1) * b]
                at = (c * band + d) * b
                done = 0
                while done < b:
                    q, offset = divmod(at + done, per)
                    count = min(b - done, per - offset)
                    at_slot = pieces // 2 - 1 - q // 2 if q % 2 else q // 2
                    (even_core, odd_core)[q % 2][at_slot, offset : offset + count, :] = block[done : done + count]
                    done += count

    @pl.when(core == 0)
    def _():
        write(keep, send)

    @pl.when(core == 1)
    def _():
        write(send, keep)


def first_kernel(a_local, a_cols, p_local, p_cols):
    fr, ka, b = a_local.shape[:3]
    acol = a_cols[0].transpose(2, 0, 1)
    pcol = p_cols[:, 0].transpose(1, 2, 0)
    chunks = 2
    vmem = pl.BlockSpec(memory_space=pltpu.VMEM)
    hbm = pl.BlockSpec(memory_space=pltpu.HBM)
    n = NC * b
    return pl.pallas_call(
        functools.partial(own_kernel, fr, ka, b, chunks),
        out_shape=[
            jax.ShapeDtypeStruct((n, n), BF16),
            jax.ShapeDtypeStruct((n, HB * b), BF16),
            jax.ShapeDtypeStruct((n, HB * b), BF16),
            jax.ShapeDtypeStruct((2, HB, 2, NC, 16, b), BF16),
        ],
        in_specs=[hbm] * 4,
        out_specs=[vmem] * 4,
        scratch_shapes=[
            pltpu.SMEM(acol.shape, jnp.int32),
            pltpu.SMEM(pcol.shape, jnp.int32),
            pltpu.VMEM(a_local.shape, BF16),
            pltpu.VMEM(p_local.shape, BF16),
            pltpu.VMEM((NC, (fr + 1) * b, b), BF16),
            pltpu.VMEM((fr * b, n), BF16),
            pltpu.SemaphoreType.DMA((3 + chunks,)),
        ],
        cost_estimate=pl.CostEstimate(flops=2_000_000_000, bytes_accessed=6_000_000, transcendentals=0),
        compiler_params=pltpu.CompilerParams(vmem_limit_bytes=40 << 20),
        name="own_part",
    )(*[pltpu.with_memory_space_constraint(x, pltpu.HBM) for x in (acol, pcol, a_local, p_local)])


def body(a_blocks, a_cols, p_blocks, p_cols):
    a_local, p_local = a_blocks[0, 0], p_blocks[0, 0]
    fr, ka, b = a_local.shape[:3]
    regions = p_cols.shape[0]
    band = 3 * NC
    pieces = lax.axis_size("grp")
    z_count = pieces // 2
    per = NC * band * b // pieces
    odd = lax.rem(lax.axis_index("agg") + lax.axis_index("grp"), 2)

    def swap(least, start):
        pairs = [
            (i * pieces + g, (i + 1) * pieces + g)
            for g in range(pieces)
            for i in range((least + g) % 2, regions - 1, 2)
        ]
        ends = lax.dynamic_slice_in_dim(p_local, start * (fr - HB), HB, 0)
        return lax.ppermute(ends, ("agg", "grp"), pairs + [(j, i) for i, j in pairs])

    first, second = swap(0, 1 - odd), swap(1, odd)

    vmem = pl.BlockSpec(memory_space=pltpu.VMEM)
    own, v_first, v_second, mask = first_kernel(a_local, a_cols, p_local, p_cols)

    keep, send = pl.pallas_call(
        functools.partial(halo_kernel, b, pieces),
        out_shape=[jax.ShapeDtypeStruct((z_count, per, b), BF16)] * 2,
        in_specs=[vmem] * 6,
        out_specs=[vmem] * 2,
        cost_estimate=pl.CostEstimate(flops=400_000_000, bytes_accessed=3_000_000, transcendentals=0),
        compiler_params=pltpu.CompilerParams(vmem_limit_bytes=20 << 20),
        name="halo_part",
    )(own, v_first, v_second, mask, first, second)

    chips = [[2 * z, 2 * z + 1] for z in range(z_count)]
    same_core = [[2 * z for z in reversed(range(z_count))], [2 * z + 1 for z in range(z_count)]]
    falling = [[2 * z + c for z in reversed(range(z_count)) for c in range(2)]]
    sent = lax.all_gather(send, "grp", axis_index_groups=chips)
    core = lax.rem(lax.axis_index("grp"), 2)
    got = lax.dynamic_index_in_dim(sent, 1 - core, 0, keepdims=False)
    pair = (keep.astype(F32) + got.astype(F32)).astype(BF16)
    mine = lax.all_to_all(pair, "grp", 0, 0, tiled=True, axis_index_groups=same_core)
    mine = mine.astype(F32).sum(0).astype(BF16)
    whole = lax.all_gather(mine, "grp", tiled=True, axis_index_groups=falling)
    return whole.reshape(NC, band, b, b).transpose(2, 0, 1, 3)[None]


def solution(mesh):
    return jax.shard_map(
        body,
        mesh=mesh,
        in_specs=(
            P("agg", "grp", None, None, None, None),
            P("agg", "grp", None, None),
            P("agg", "grp", None, None, None, None),
            P(None, "grp", None, None),
        ),
        out_specs=P("agg", None, None, None, None),
        check_vma=False,
    )
```
